32 devices in a mesh: dp: 4 (over z), fsdp: 8 (over y, x, core).
Axes of the slice: x: 2, y: 2, z: 4, core: 2. Of those that a mesh axis runs over, the one named last changes fastest.
Arguments:
- layer_input: bfloat16 [2, 6144, 2048], P(None, ('dp', 'fsdp')), may hold values from -6 to 6
- segment_ids: int32 [2, 6144], P(None, ('dp', 'fsdp')), may hold values from 0 to 383, as said below
- live_counts: int32 [2, 32], P(None, ('dp', 'fsdp')), may hold values from 96 to 192, as said below
- w_query: bfloat16 [2048, 2048], P(('dp', 'fsdp')), may hold values from -0.125 to 0.125
- w_key: bfloat16 [2048, 256], P(('dp', 'fsdp')), may hold values from -0.125 to 0.125
- w_value: bfloat16 [2048, 256], P(('dp', 'fsdp')), may hold values from -0.125 to 0.125
- w_out: bfloat16 [2048, 2048], P(('dp', 'fsdp')), may hold values from -0.375 to 0.375
- w_gate: bfloat16 [2048, 5632], P(('dp', 'fsdp')), may hold values from -0.125 to 0.125
- w_up: bfloat16 [2048, 5632], P(('dp', 'fsdp')), may hold values from -0.125 to 0.125
- w_down: bfloat16 [5632, 2048], P(('dp', 'fsdp')), may hold values from -0.078125 to 0.078125
- attn_gain: bfloat16 [2048], P(('dp', 'fsdp')), may hold values from 0.5 to 1.5
- mlp_gain: bfloat16 [2048], P(('dp', 'fsdp')), may hold values from 0.5 to 1.5
- out_grad: bfloat16 [2, 6144, 2048], P(None, ('dp', 'fsdp')), may hold values from -6 to 6
Outputs:
- layer_output: bfloat16 [2, 6144, 2048], P(None, ('dp', 'fsdp'))
- input_grad: float32 [2, 6144, 2048], P(None, ('dp', 'fsdp'))
- grad_w_query: float32 [2048, 2048], P(('dp', 'fsdp'))
- grad_w_key: float32 [2048, 256], P(('dp', 'fsdp'))
- grad_w_value: float32 [2048, 256], P(('dp', 'fsdp'))
- grad_w_out: float32 [2048, 2048], P(('dp', 'fsdp'))
- grad_w_gate: float32 [2048, 5632], P(('dp', 'fsdp'))
- grad_w_up: float32 [2048, 5632], P(('dp', 'fsdp'))
- grad_w_down: float32 [5632, 2048], P(('dp', 'fsdp'))
- grad_attn_gain: float32 [2048], P(('dp', 'fsdp'))
- grad_mlp_gain: float32 [2048], P(('dp', 'fsdp'))
The draws below stay inside these ranges and needn't reach their ends.
Inputs may be any that keep to these rules, and one draw needn't show every extreme that they name: `segment_ids`: within each device's block segment numbers never fall; live slots come first, with segment numbers from 0, and padding slot at place i of the block has the number 192 + i. Some block is one whole sequence of 192 live tokens. `live_counts`: live tokens of each device's block.
All inputs are finite; a program needn't handle non-finite values.
Results may differ from the reference program's by a relative error of at most 0.013.
Values may be sent and summed in bfloat16 or wider, within the bound.
No kernel may reach another device: no remote copies, remote signals or barrier semaphores. Data moves between devices by JAX's collectives and lax.ppermute only.
A program may use at most 384 MiB of HBM per device.

```python
import jax
import jax.numpy as jnp
from jax import lax

D = 2048
HEADS = 32
KV_HEADS = 4
FF = 5632
HEAD_DIM = 64
TOK = 192
MICRO = 2
TOKENS = 6144
N_DP = 4
N_FSDP = 8


def segment_plan(key):
    base = jax.random.fold_in(key, 7)
    key_count, key_whole, key_break = jax.random.split(base, 3)
    total = N_DP * N_FSDP
    column = jnp.arange(total, dtype=jnp.int32)[None, :]
    drawn = jax.random.randint(key_count, (MICRO, total), TOK // 2, TOK + 1)
    live = jnp.where(column == 0, TOK, jnp.where(column == 1, TOK // 2, drawn))
    whole_doc = (jax.random.randint(key_whole, (MICRO, total), 0, 4) == 0) | (column == 0)
    place = jnp.arange(TOK, dtype=jnp.int32)[None, None, :]
    breaks = jax.random.randint(key_break, (MICRO, total, TOK), 0, 16) == 0
    breaks = breaks & (place > 0) & jnp.logical_not(whole_doc[:, :, None])
    segment = jnp.cumsum(breaks.astype(jnp.int32), axis=-1)
    segment = jnp.where(place < live[:, :, None], segment, TOK + place)
    return (live.astype(jnp.int32), segment.reshape(MICRO, total * TOK).astype(jnp.int32))


def draw_segment_ids(key, part):
    return segment_plan(key)[1]


def draw_live_counts(key, part):
    return segment_plan(key)[0]


def raised(values, stream_key, source, target, parts, factor):
    def block_of(axis_at):
        return (jnp.arange(values.shape[axis_at]) // (values.shape[axis_at] // parts)).reshape((-1,) + (1,) * (values.ndim - 1 - axis_at))

    one_side = jax.random.permutation(stream_key, parts)[block_of(target)]
    other_side = (block_of(target) + parts // 2) % parts
    return jnp.where((block_of(source) == one_side) | (block_of(source) == other_side), factor * values, values)


def level_of(stream_key, dims, cuts, least, high):
    def one(position, shards_of):
        steps = jax.random.uniform(jax.random.fold_in(jax.random.fold_in(stream_key, 6), position), (shards_of,), jnp.float32, least / len(cuts), high / len(cuts))
        return jnp.repeat(jnp.exp(steps), dims[position] // shards_of).reshape((-1,) + (1,) * (len(dims) - position - 1))

    level = one(*cuts[0])
    for cut in cuts[1:]:
        level = level * one(*cut)
    return level


def centred(own_key, extent, scale, bound, cuts=(), kind=jnp.bfloat16):
    entries = jax.random.normal(own_key, extent, jnp.float32) * scale
    if len(cuts) > 0:
        entries = level_of(own_key, extent, cuts, -0.22, 0.18) * entries
    return jnp.clip(entries, min=-bound, max=bound).astype(kind)


def heavy_noise(own_key, dims, deviation, bound, cuts, heavy, kind=jnp.bfloat16):
    array = deviation * jax.random.normal(own_key, dims, jnp.float32)
    if cuts:
        array = array * level_of(own_key, dims, cuts, -0.22, 0.18)
    return jnp.clip(raised(array, jax.random.fold_in(own_key, 3), *heavy), -bound, bound).astype(kind)


def setup_inputs(seed: int = 0) -> dict:
    key_of = jax.random.split(jax.random.key(seed), 14)
    return {
        "layer_input": heavy_noise(key_of[0], (MICRO, TOKENS, D), 1.0, 6.0, ((1, 32),), (1, 2, 32, 2.75)),
        "segment_ids": draw_segment_ids(jax.random.fold_in(key_of[13], 71), 0),
        "live_counts": draw_live_counts(jax.random.fold_in(key_of[13], 71), 0),
        "w_query": centred(key_of[3], (D, HEADS * HEAD_DIM), D ** -0.5, 0.125, ((0, 32),)),
        "w_key": centred(key_of[4], (D, KV_HEADS * HEAD_DIM), D ** -0.5, 0.125, ((0, 32),)),
        "w_value": centred(key_of[5], (D, KV_HEADS * HEAD_DIM), D ** -0.5, 0.125, ((0, 32),)),
        "w_out": centred(key_of[6], (HEADS * HEAD_DIM, D), (D // 8) ** -0.5, 0.375, ((0, 32),)),
        "w_gate": centred(key_of[7], (D, FF), D ** -0.5, 0.125, ((0, 32),)),
        "w_up": centred(key_of[8], (D, FF), D ** -0.5, 0.125, ((0, 32),)),
        "w_down": centred(key_of[9], (FF, D), FF ** -0.5, 0.078125, ((0, 32),)),
        "attn_gain": jnp.clip(1.0 + 0.1 * jax.random.normal(key_of[10], (D,), jnp.float32), 0.5, 1.5).astype(jnp.bfloat16),
        "mlp_gain": jnp.clip(1.0 + 0.1 * jax.random.normal(key_of[11], (D,), jnp.float32), 0.5, 1.5).astype(jnp.bfloat16),
        "out_grad": centred(key_of[12], (MICRO, TOKENS, D), 1.0, 6.0, ((1, 32),)),
    }


EPS = 1e-05
HIGH = lax.Precision.HIGHEST

@jax.custom_vjp
def low(v):
    return lax.optimization_barrier(v.astype(jnp.bfloat16)).astype(jnp.float32)

@jax.custom_vjp
def low_back(v):
    return v

def low_keep(v):
    return (low(v), None)

def low_pass(kept, grad):
    return (grad,)

def back_keep(v):
    return (v, None)

def back_low(kept, grad):
    return (low(grad),)
low.defvjp(low_keep, low_pass)
low_back.defvjp(back_keep, back_low)

def product(left, right):
    return jnp.dot(left, right, precision=HIGH)

def rms_scale(value, gain):
    return value * lax.rsqrt(lax.optimization_barrier(jnp.mean(value * value, axis=-1, keepdims=True)) + EPS) * gain

def positions(segment):
    place = jnp.arange(segment.shape[0], dtype=jnp.int32)
    before = jnp.concatenate([segment[:1] - 1, segment[:-1]])
    start = lax.cummax(jnp.where(segment != before, place, 0), axis=0)
    return place - start

def rope_tables(pos):
    steps = jnp.arange(HEAD_DIM // 2, dtype=jnp.int32).astype(jnp.float32)
    freq = 10000.0 ** (-2.0 * steps / HEAD_DIM)
    angle = pos.astype(jnp.float32)[:, None] * freq[None, :]
    cos_half = jnp.cos(angle)
    sin_half = jnp.sin(angle)
    return (jnp.concatenate([cos_half, cos_half], axis=-1), jnp.concatenate([sin_half, sin_half], axis=-1))

def rotate(value, cos_t, sin_t):
    half = HEAD_DIM // 2
    turned = jnp.concatenate([-value[..., half:], value[..., :half]], axis=-1)
    return value * cos_t[:, None, :] + turned * sin_t[:, None, :]

def attend(pieces):
    query, keys, values, segment = pieces
    span = jnp.arange(TOK, dtype=jnp.int32)
    cos_t, sin_t = rope_tables(positions(segment))
    q_rot = low(rotate(query, cos_t, sin_t)).reshape(TOK, KV_HEADS, HEADS // KV_HEADS, HEAD_DIM)
    k_rot = low(rotate(keys, cos_t, sin_t))
    scores = low_back(jnp.einsum('qkgd,skd->kgqs', q_rot, k_rot, precision=HIGH) * HEAD_DIM ** (-0.5))
    allow = (segment[:, None] == segment[None, :]) & (span[None, :] <= span[:, None])
    probs = low(jax.nn.softmax(jnp.where(allow, scores, -1000000000.0), axis=-1))
    mixed = jnp.einsum('kgqs,skd->qkgd', probs, values, precision=HIGH)
    return mixed.reshape(TOK, HEADS * HEAD_DIM)

def forward(inputs, w_query, w_key, w_value, w_out, w_gate, w_up, w_down, attn_gain, mlp_gain, seg_flat, valid):
    h1 = low(rms_scale(inputs, attn_gain))
    query = low_back(product(h1, w_query)).reshape(-1, TOK, HEADS, HEAD_DIM)
    keys = low_back(product(h1, w_key)).reshape(-1, TOK, KV_HEADS, HEAD_DIM)
    values = low(low_back(product(h1, w_value))).reshape(-1, TOK, KV_HEADS, HEAD_DIM)
    mixed = lax.map(jax.checkpoint(attend), (query, keys, values, seg_flat.reshape(-1, TOK)))
    mixed = low(low_back(mixed.reshape(-1, HEADS * HEAD_DIM)))
    hidden = inputs + low_back(product(mixed, w_out))
    h2 = low(rms_scale(hidden, mlp_gain))
    gate = low_back(product(h2, w_gate))
    upward = low_back(product(h2, w_up))
    inner = low(jax.nn.silu(gate) * upward)
    result = hidden + low_back(product(inner, w_down))
    return result * valid

def reference(layer_input, segment_ids, live_counts, w_query, w_key, w_value, w_out, w_gate, w_up, w_down, attn_gain, mlp_gain, out_grad):
    rows = MICRO * TOKENS
    place = jnp.arange(TOKENS, dtype=jnp.int32) % TOK
    owner_count = jnp.repeat(live_counts, TOK, axis=1)
    valid = (place[None, :] < owner_count).astype(jnp.float32).reshape(rows, 1)
    seg_flat = segment_ids.reshape(rows)
    weights = (w_query.astype(jnp.float32), w_key.astype(jnp.float32), w_value.astype(jnp.float32), w_out.astype(jnp.float32), w_gate.astype(jnp.float32), w_up.astype(jnp.float32), w_down.astype(jnp.float32), attn_gain.astype(jnp.float32), mlp_gain.astype(jnp.float32))

    def layer(inputs, *params):
        return forward(inputs, *params, seg_flat, valid)
    result, pull = jax.vjp(layer, layer_input.reshape(rows, D).astype(jnp.float32), *weights)
    grads = pull(out_grad.reshape(rows, D).astype(jnp.float32))
    layer_output = result.astype(jnp.bfloat16).reshape(MICRO, TOKENS, D)
    return (layer_output, grads[0].reshape(MICRO, TOKENS, D), grads[1], grads[2], grads[3], grads[4], grads[5], grads[6], grads[7], grads[8], grads[9])
```

```python
import jax
import jax.numpy as jnp
from jax import lax
from jax.experimental import pallas as pl
from jax.experimental.pallas import tpu as pltpu
from jax.sharding import Mesh, PartitionSpec as P

HEADS = 32
KV_HEADS = 4
HEAD_DIM = 64
MICRO = 2
RANKS = 4
SCALING = HEAD_DIM ** (-0.5)
EPS = 1e-05
NEG = -1000000000.0
BF16 = jnp.bfloat16
F32 = jnp.float32


def contract(left, right, dims):
    return lax.dot_general(left, right, (dims, ((), ())), preferred_element_type=F32)


def inner_rows(left, right):
    return contract(left, right, ((0,), (0,)))


def against(left, weight):
    return contract(left, weight, ((1,), (1,)))


def forward_dot(left, weight):
    return contract(left, weight, ((1,), (0,)))


def turned_half(value):
    lane = lax.broadcasted_iota(jnp.int32, value.shape, 1)
    width = value.shape[1]
    ahead = pltpu.roll(value, width - HEAD_DIM // 2, axis=1)
    behind = pltpu.roll(value, HEAD_DIM // 2, axis=1)
    return jnp.where(lane % HEAD_DIM < HEAD_DIM // 2, -ahead, behind)


def stacked_heads(pair):
    return jnp.concatenate([pair[:, :HEAD_DIM], pair[:, HEAD_DIM:]], axis=0)


def paired_heads(tall):
    rows = tall.shape[0] // 2
    return jnp.concatenate([tall[:rows], tall[rows:]], axis=1)


def allowed_pairs(segc_ref, segr_ref):
    segc, segr = segc_ref[0], segr_ref[0]
    rows = segc.shape[0]
    later = lax.broadcasted_iota(jnp.int32, (rows, rows), 0)
    earlier = lax.broadcasted_iota(jnp.int32, (rows, rows), 1)
    allow = jnp.logical_and(segc == segr, earlier <= later)
    return jnp.where(allow, 0.0, NEG)


def head_probs(tall_q, key, bias):
    scores = contract(tall_q, key, ((1,), (1,))) * SCALING
    rows = bias.shape[0]
    scores = jnp.concatenate(
        [
            jnp.where(bias < 0.0, bias, scores[:rows]),
            jnp.where(bias < 0.0, bias, scores[rows:]),
        ],
        axis=0,
    )
    top = jnp.max(scores, axis=1, keepdims=True)
    grown = jnp.exp(scores - top)
    return grown / jnp.sum(grown, axis=1, keepdims=True)


def attend_kernel(width, side, qkv_ref, tab_ref, segc_ref, segr_ref, o_ref, qr_ref, kr_ref, v_ref):
    cos_t, sin_t = tab_ref[:, :128], tab_ref[:, 128:]
    bias = allowed_pairs(segc_ref, segr_ref)
    kinds = []
    for start in range(0, side, 128):
        piece = qkv_ref[:, width + start : width + start + 128]
        piece = (piece * cos_t + turned_half(piece) * sin_t).astype(BF16)
        kr_ref[:, start : start + 128] = piece
        kinds.append(piece)
    values = qkv_ref[:, width + side :].astype(BF16)
    v_ref[...] = values
    for group in range(width // 128):
        piece = qkv_ref[:, group * 128 : group * 128 + 128]
        piece = (piece * cos_t + turned_half(piece) * sin_t).astype(BF16)
        qr_ref[:, group * 128 : group * 128 + 128] = piece
        at = (group % 2) * HEAD_DIM
        key = kinds[group // 2][:, at : at + HEAD_DIM]
        probs = head_probs(stacked_heads(piece), key, bias)
        value = values[:, group * HEAD_DIM : group * HEAD_DIM + HEAD_DIM]
        mixed = contract(probs.astype(BF16), value, ((1,), (0,)))
        o_ref[:, group * 128 : group * 128 + 128] = paired_heads(mixed).astype(BF16)


def attend_back_kernel(
    width, side, do_ref, qr_ref, kr_ref, v_ref, tab_ref, segc_ref, segr_ref, out_ref
):
    cos_t, sin_t = tab_ref[:, :128], tab_ref[:, 128:]
    bias = allowed_pairs(segc_ref, segr_ref)
    key_grads = []
    value_grads = []
    for group in range(width // 128):
        tall_q = stacked_heads(qr_ref[:, group * 128 : group * 128 + 128])
        tall_do = stacked_heads(do_ref[:, group * 128 : group * 128 + 128])
        here = slice(group * HEAD_DIM, group * HEAD_DIM + HEAD_DIM)
        key, value = kr_ref[:, here], v_ref[:, here]
        probs = head_probs(tall_q, key, bias)
        value_grads.append(contract(probs.astype(BF16), tall_do, ((0,), (0,))))
        grad_probs = contract(tall_do, value, ((1,), (1,)))
        kept = jnp.sum(grad_probs * probs, axis=1, keepdims=True)
        grad_scores = (probs * (grad_probs - kept)).astype(BF16)
        grad_q = paired_heads(contract(grad_scores, key, ((1,), (0,)))) * SCALING
        grad_q = grad_q * cos_t - turned_half(grad_q) * sin_t
        out_ref[:, group * 128 : group * 128 + 128] = grad_q.astype(BF16)
        key_grads.append(contract(grad_scores, tall_q, ((0,), (0,))) * SCALING)
    for index in range(side // 128):
        both = jnp.concatenate([key_grads[2 * index], key_grads[2 * index + 1]], axis=1)
        both = both * cos_t - turned_half(both) * sin_t
        at = width + index * 128
        out_ref[:, at : at + 128] = both.astype(BF16)
        both = jnp.concatenate([value_grads[2 * index], value_grads[2 * index + 1]], axis=1)
        at = width + side + index * 128
        out_ref[:, at : at + 128] = both.astype(BF16)


def rows_spec(rows, columns):
    return pl.BlockSpec((rows, columns), lambda block: (block, 0))


def segment_specs(rows):
    return [
        pl.BlockSpec((1, rows, 1), lambda block: (block, 0, 0)),
        pl.BlockSpec((1, 1, rows), lambda block: (block, 0, 0)),
    ]


def attend(qkv, table, segments, width, side):
    blocks, rows = segments.shape

    def kernel(*refs):
        attend_kernel(width, side, *refs)

    return pl.pallas_call(
        kernel,
        grid=(blocks,),
        in_specs=[rows_spec(rows, qkv.shape[1]), rows_spec(rows, 256)] + segment_specs(rows),
        out_specs=[
            rows_spec(rows, width),
            rows_spec(rows, width),
            rows_spec(rows, side),
            rows_spec(rows, side),
        ],
        out_shape=[
            jax.ShapeDtypeStruct((blocks * rows, columns), BF16)
            for columns in (width, width, side, side)
        ],
        name="attend",
    )(qkv, table, segments[:, :, None], segments[:, None, :])


def attend_back(grad_mixed, q_rot, k_rot, values, table, segments, width, side):
    blocks, rows = segments.shape

    def kernel(*refs):
        attend_back_kernel(width, side, *refs)

    return pl.pallas_call(
        kernel,
        grid=(blocks,),
        in_specs=[
            rows_spec(rows, width),
            rows_spec(rows, width),
            rows_spec(rows, side),
            rows_spec(rows, side),
            rows_spec(rows, 256),
        ]
        + segment_specs(rows),
        out_specs=rows_spec(rows, width + 2 * side),
        out_shape=jax.ShapeDtypeStruct((blocks * rows, width + 2 * side), BF16),
        name="attend_back",
    )(grad_mixed, q_rot, k_rot, values, table, segments[:, :, None], segments[:, None, :])


def rope_table(segments):
    rows = segments.shape[1]
    span = jnp.arange(rows, dtype=jnp.int32)
    same = (segments[:, :, None] == segments[:, None, :]) & (span[None, :] < span[:, None])
    pos = jnp.sum(same.astype(jnp.int32), axis=2).reshape(-1)
    steps = jnp.arange(HEAD_DIM // 2, dtype=jnp.int32).astype(F32)
    freq = 10000.0 ** (-2.0 * steps / HEAD_DIM)
    angle = pos.astype(F32)[:, None] * freq[None, :]
    cos_half, sin_half = jnp.cos(angle), jnp.sin(angle)
    return jnp.concatenate([cos_half] * 4 + [sin_half] * 4, axis=1)


def swap(value, axis):
    return lax.ppermute(value, axis, [(0, 1), (1, 0)])


def gather_group(value):
    across = swap(value, "x")
    beside = swap(value, "c")
    beside_across = swap(across, "c")
    return jnp.concatenate([value, across, beside, beside_across], axis=0)


def reduce_group(product, left):
    quarter = left.shape[0] // RANKS
    far = product(left[2 * quarter :]).astype(BF16)
    from_core = swap(far, "c")
    across = product(left[quarter : 2 * quarter]) + from_core[quarter:].astype(F32)
    from_chip = swap(across.astype(BF16), "x")
    own = product(left[:quarter]) + from_core[:quarter].astype(F32)
    return own + from_chip.astype(F32)


def gather_rows(value):
    return lax.all_gather(value, ("dp", "y"), axis=0, tiled=True)


def scatter_rows(value):
    return lax.psum_scatter(value, ("dp", "y"), scatter_dimension=0, tiled=True)


def exchange(value):
    return lax.all_to_all(value, ("x", "c"), 0, 0, tiled=True)


def by_rank(weight, piece):
    rows, columns = weight.shape
    parts = weight.reshape(rows, columns // (RANKS * piece), RANKS, piece)
    return parts.transpose(2, 0, 1, 3).reshape(RANKS * rows, columns // RANKS)


def from_ranks(value, piece):
    ranks, rows, columns = value.shape
    parts = value.reshape(ranks, rows, columns // piece, piece)
    return parts.transpose(1, 2, 0, 3).reshape(rows, ranks * columns)


def unit(value):
    scale = lax.rsqrt(jnp.mean(value * value, axis=-1, keepdims=True) + EPS)
    return value * scale, scale


def unit_back(normed, scale, grad):
    return scale * (grad - normed * jnp.mean(grad * normed, axis=-1, keepdims=True))


def layer(
    layer_input,
    segment_ids,
    live_counts,
    w_query,
    w_key,
    w_value,
    w_out,
    w_gate,
    w_up,
    w_down,
    attn_gain,
    mlp_gain,
    out_grad,
):
    micro, rows, model = layer_input.shape
    tokens = micro * rows
    owned = w_query.shape[0]
    piece = w_down.shape[0]
    width = w_query.shape[1] // RANKS
    side = w_key.shape[1]
    hidden_units = w_gate.shape[1] // RANKS
    span = jnp.arange(rows, dtype=jnp.int32)
    valid = (span[None, :] < live_counts).astype(F32).reshape(tokens, 1)

    gain1 = attn_gain.astype(F32)[:, None]
    gain2 = mlp_gain.astype(F32)[:, None]
    scaled = lambda weight, gain: (weight.astype(F32) * gain).astype(BF16)
    side_weights = jnp.concatenate([scaled(w_key, gain1), scaled(w_value, gain1)], axis=1)
    qkv_sent = jnp.concatenate(
        [by_rank(scaled(w_query, gain1), HEAD_DIM), jnp.tile(side_weights, (RANKS, 1))], axis=1
    )
    gu_sent = jnp.concatenate(
        [by_rank(scaled(w_gate, gain2), piece), by_rank(scaled(w_up, gain2), piece)], axis=1
    )
    w_qkv = gather_rows(exchange(qkv_sent))
    wo = gather_rows(w_out)
    w_gu = gather_rows(exchange(gu_sent))
    wd = gather_rows(w_down)

    segments = gather_group(segment_ids)
    table = rope_table(segments)

    inputs = layer_input.reshape(tokens, model).astype(F32)
    n1, r1 = unit(inputs)
    n1_all = gather_group(n1.astype(BF16))
    error = out_grad.reshape(tokens, model).astype(F32) * valid
    error_all = gather_group(error.astype(BF16))

    qkv = forward_dot(n1_all, w_qkv)
    mixed, q_rot, k_rot, values = attend(qkv, table, segments, width, side)
    hidden = inputs + reduce_group(lambda left: forward_dot(left, wo), mixed)

    n2, r2 = unit(hidden)
    n2_all = gather_group(n2.astype(BF16))
    gate_up = forward_dot(n2_all, w_gu)
    gate, upward = gate_up[:, :hidden_units], gate_up[:, hidden_units:]
    sigma = jax.nn.sigmoid(gate)
    silu_gate = gate * sigma
    inner = (silu_gate * upward).astype(BF16)
    result = hidden + reduce_group(lambda left: forward_dot(left, wd), inner)
    layer_output = (result * valid).astype(BF16).reshape(micro, rows, model)

    grad_wd = scatter_rows(inner_rows(inner, error_all).astype(BF16)).astype(F32)
    grad_inner = against(error_all, wd)
    grad_gate = grad_inner * upward * (sigma + gate * sigma * (1.0 - sigma))
    grad_up = grad_inner * silu_gate
    grad_gu = jnp.concatenate([grad_gate.astype(BF16), grad_up.astype(BF16)], axis=1)
    gu_raw = exchange(scatter_rows(inner_rows(n2_all, grad_gu).astype(BF16)))
    grad_n2 = reduce_group(lambda left: against(left, w_gu), grad_gu)
    grad_hidden = error + unit_back(n2, r2, grad_n2)
    hidden_all = gather_group(grad_hidden.astype(BF16))
    grad_mixed = against(hidden_all, wo).astype(BF16)
    grad_wo = scatter_rows(inner_rows(mixed, hidden_all).astype(BF16)).astype(F32)
    grad_qkv = attend_back(grad_mixed, q_rot, k_rot, values, table, segments, width, side)
    qkv_raw = exchange(scatter_rows(inner_rows(n1_all, grad_qkv).astype(BF16)))
    grad_n1 = reduce_group(lambda left: against(left, w_qkv), grad_qkv)
    input_grad = (grad_hidden + unit_back(n1, r1, grad_n1)).reshape(micro, rows, model)

    gu_raw = gu_raw.reshape(RANKS, owned, 2 * hidden_units).astype(F32)
    raw_gate = from_ranks(gu_raw[:, :, :hidden_units], piece)
    raw_up = from_ranks(gu_raw[:, :, hidden_units:], piece)
    qkv_raw = qkv_raw.reshape(RANKS, owned, width + 2 * side).astype(F32)
    raw_query = from_ranks(qkv_raw[:, :, :width], HEAD_DIM)
    raw_side = jnp.sum(qkv_raw[:, :, width:], axis=0)
    raw_key, raw_value = raw_side[:, :side], raw_side[:, side:]
    row_dot = lambda raw, weight: jnp.sum(raw * weight.astype(F32), axis=1)
    grad_gain1 = row_dot(raw_query, w_query) + row_dot(raw_key, w_key) + row_dot(raw_value, w_value)
    grad_gain2 = row_dot(raw_gate, w_gate) + row_dot(raw_up, w_up)
    return (
        layer_output,
        input_grad,
        raw_query * gain1,
        raw_key * gain1,
        raw_value * gain1,
        grad_wo,
        raw_gate * gain2,
        raw_up * gain2,
        grad_wd,
        grad_gain1,
        grad_gain2,
    )


def positions(segment):
    place = jnp.arange(segment.shape[0], dtype=jnp.int32)
    before = jnp.concatenate([segment[:1] - 1, segment[:-1]])
    start = lax.cummax(jnp.where(segment != before, place, 0), axis=0)
    return place - start


def rope_pair(pos):
    steps = jnp.arange(HEAD_DIM // 2, dtype=jnp.int32).astype(F32)
    freq = 10000.0 ** (-2.0 * steps / HEAD_DIM)
    angle = pos.astype(F32)[:, None] * freq[None, :]
    cos_half, sin_half = jnp.cos(angle), jnp.sin(angle)
    return (
        jnp.concatenate([cos_half, cos_half], axis=-1),
        jnp.concatenate([sin_half, sin_half], axis=-1),
    )


def rotate(value, cos_t, sin_t):
    half = HEAD_DIM // 2
    turned = jnp.concatenate([-value[..., half:], value[..., :half]], axis=-1)
    return value * cos_t[:, None, :] + turned * sin_t[:, None, :]


def plain_layer(
    layer_input,
    segment_ids,
    live_counts,
    w_query,
    w_key,
    w_value,
    w_out,
    w_gate,
    w_up,
    w_down,
    attn_gain,
    mlp_gain,
    out_grad,
):
    axes = ("dp", "y", "x", "c")
    rows = layer_input.shape[1]
    group = HEADS // KV_HEADS
    width = HEADS * HEAD_DIM
    span = jnp.arange(rows, dtype=jnp.int32)
    whole = lambda value: lax.all_gather(value, axes, axis=0, tiled=True)
    wq, wk, wv, wo, g1 = [whole(w) for w in (w_query, w_key, w_value, w_out, attn_gain)]
    wg, wu, wd, g2 = [whole(w) for w in (w_gate, w_up, w_down, mlp_gain)]
    gain1, gain2 = g1.astype(F32), g2.astype(F32)
    outputs, input_grads, kept = [], [], []
    gain_sums = [0.0, 0.0]
    for micro in range(MICRO):
        segment = segment_ids[micro]
        valid = (span < live_counts[micro, 0]).astype(F32)[:, None]
        cos_t, sin_t = rope_pair(positions(segment))
        allow = (segment[:, None] == segment[None, :]) & (span[None, :] <= span[:, None])
        inputs = layer_input[micro].astype(F32)
        n1, r1 = unit(inputs)
        h1 = (n1 * gain1).astype(BF16)
        query = forward_dot(h1, wq).reshape(rows, HEADS, HEAD_DIM)
        keys = forward_dot(h1, wk).reshape(rows, KV_HEADS, HEAD_DIM)
        values = forward_dot(h1, wv).astype(BF16).reshape(rows, KV_HEADS, HEAD_DIM)
        q_rot = rotate(query, cos_t, sin_t).astype(BF16).reshape(rows, KV_HEADS, group, HEAD_DIM)
        k_rot = rotate(keys, cos_t, sin_t).astype(BF16)
        scores = jnp.einsum("qkgd,skd->kgqs", q_rot, k_rot, preferred_element_type=F32) * SCALING
        probs = jax.nn.softmax(jnp.where(allow, scores, NEG), axis=-1)
        probs_b = probs.astype(BF16)
        mixed = jnp.einsum("kgqs,skd->qkgd", probs_b, values, preferred_element_type=F32)
        mixed = mixed.reshape(rows, width).astype(BF16)
        hidden = inputs + forward_dot(mixed, wo)
        n2, r2 = unit(hidden)
        h2 = (n2 * gain2).astype(BF16)
        gate, upward = forward_dot(h2, wg), forward_dot(h2, wu)
        sigma = jax.nn.sigmoid(gate)
        inner = (gate * sigma * upward).astype(BF16)
        outputs.append(((hidden + forward_dot(inner, wd)) * valid).astype(BF16))
        error = out_grad[micro].astype(F32) * valid
        error_low = error.astype(BF16)
        grad_inner = against(error_low, wd)
        grad_gate = (grad_inner * upward * (sigma + gate * sigma * (1.0 - sigma))).astype(BF16)
        grad_up = (grad_inner * gate * sigma).astype(BF16)
        grad_h2 = against(grad_gate, wg) + against(grad_up, wu)
        gain_sums[1] += jnp.sum(n2 * grad_h2, axis=0)
        grad_hidden = error + unit_back(n2, r2, grad_h2 * gain2)
        grad_low = grad_hidden.astype(BF16)
        grad_mixed = against(grad_low, wo).astype(BF16).reshape(rows, KV_HEADS, group, HEAD_DIM)
        grad_probs = jnp.einsum("qkgd,skd->kgqs", grad_mixed, values, preferred_element_type=F32)
        kept_sum = jnp.sum(grad_probs * probs, axis=-1, keepdims=True)
        grad_scores = (probs * (grad_probs - kept_sum)).astype(BF16)
        grad_values = jnp.einsum("kgqs,qkgd->skd", probs_b, grad_mixed, preferred_element_type=F32)
        grad_values = grad_values.astype(BF16).reshape(rows, KV_HEADS * HEAD_DIM)
        grad_q = jnp.einsum("kgqs,skd->qkgd", grad_scores, k_rot, preferred_element_type=F32)
        grad_k = jnp.einsum("kgqs,qkgd->skd", grad_scores, q_rot, preferred_element_type=F32)
        grad_q = rotate(grad_q.reshape(rows, HEADS, HEAD_DIM) * SCALING, cos_t, -sin_t)
        grad_q = grad_q.astype(BF16).reshape(rows, width)
        grad_k = rotate(grad_k * SCALING, cos_t, -sin_t)
        grad_k = grad_k.astype(BF16).reshape(rows, KV_HEADS * HEAD_DIM)
        grad_h1 = against(grad_q, wq) + against(grad_k, wk) + against(grad_values, wv)
        gain_sums[0] += jnp.sum(n1 * grad_h1, axis=0)
        input_grads.append(grad_hidden + unit_back(n1, r1, grad_h1 * gain1))
        kept.append(
            (h1, grad_q, grad_k, grad_values, mixed, grad_low)
            + (h2, grad_gate, grad_up, inner, error_low)
        )
    joined = [jnp.concatenate(items, axis=0) for items in zip(*kept)]
    scatter = lambda value: lax.psum_scatter(value, axes, scatter_dimension=0, tiled=True)
    pairs = ((0, 1), (0, 2), (0, 3), (4, 5), (6, 7), (6, 8), (9, 10))
    grads = [scatter(inner_rows(joined[left], joined[right])) for left, right in pairs]
    return (
        jnp.stack(outputs, axis=0),
        jnp.stack(input_grads, axis=0),
        *grads,
        scatter(gain_sums[0]),
        scatter(gain_sums[1]),
    )


def solution(mesh):
    inner, outer = mesh.shape["fsdp"], mesh.shape["dp"]
    grid = Mesh(mesh.devices.reshape(outer, inner // RANKS, 2, 2), ("dp", "y", "x", "c"))
    every = ("dp", "y", "x", "c")
    tokens = P(None, every, None)
    flat = P(None, every)
    weight = P(every, None)
    gain = P(every)
    in_specs = (tokens, flat, flat) + (weight,) * 7 + (gain, gain, tokens)
    out_specs = (tokens, tokens) + (weight,) * 7 + (gain, gain)

    def step(*args):
        whole_heads = args[6].shape[0] == HEAD_DIM * mesh.size
        body = layer if whole_heads else plain_layer
        return jax.shard_map(
            body, mesh=grid, in_specs=in_specs, out_specs=out_specs, check_vma=False
        )(*args)

    return step
```

```python
import jax
import jax.numpy as jnp
from jax import lax
from jax.experimental import pallas as pl
from jax.experimental.pallas import tpu as pltpu
from jax.sharding import Mesh, PartitionSpec as P

HEADS = 32
KV_HEADS = 4
HEAD_DIM = 64
MICRO = 2
RANKS = 4
SCALING = HEAD_DIM ** (-0.5)
EPS = 1e-05
NEG = -1000000000.0
BF16 = jnp.bfloat16
F32 = jnp.float32


def contract(left, right, dims):
    return lax.dot_general(left, right, (dims, ((), ())), preferred_element_type=F32)


def inner_rows(left, right):
    return contract(left, right, ((0,), (0,)))


def against(left, weight):
    return contract(left, weight, ((1,), (1,)))


def forward_dot(left, weight):
    return contract(left, weight, ((1,), (0,)))


def turned_half(value):
    lane = lax.broadcasted_iota(jnp.int32, value.shape, 1)
    width = value.shape[1]
    ahead = pltpu.roll(value, width - HEAD_DIM // 2, axis=1)
    behind = pltpu.roll(value, HEAD_DIM // 2, axis=1)
    return jnp.where(lane % HEAD_DIM < HEAD_DIM // 2, -ahead, behind)


def stacked_heads(pair):
    return jnp.concatenate([pair[:, :HEAD_DIM], pair[:, HEAD_DIM:]], axis=0)


def paired_heads(tall):
    rows = tall.shape[0] // 2
    return jnp.concatenate([tall[:rows], tall[rows:]], axis=1)


def allowed_pairs(segc_ref, segr_ref):
    segc, segr = segc_ref[0], segr_ref[0]
    rows = segc.shape[0]
    later = lax.broadcasted_iota(jnp.int32, (rows, rows), 0)
    earlier = lax.broadcasted_iota(jnp.int32, (rows, rows), 1)
    allow = jnp.logical_and(segc == segr, earlier <= later)
    return jnp.where(allow, 0.0, NEG)


def head_probs(tall_q, key, bias):
    scores = contract(tall_q, key, ((1,), (1,))) * SCALING
    rows = bias.shape[0]
    scores = jnp.concatenate(
        [
            jnp.where(bias < 0.0, bias, scores[:rows]),
            jnp.where(bias < 0.0, bias, scores[rows:]),
        ],
        axis=0,
    )
    top = jnp.max(scores, axis=1, keepdims=True)
    grown = jnp.exp(scores - top)
    return grown / jnp.sum(grown, axis=1, keepdims=True)


def attend_kernel(width, side, qkv_ref, tab_ref, segc_ref, segr_ref, o_ref, qr_ref, kr_ref, v_ref):
    cos_t, sin_t = tab_ref[:, :128], tab_ref[:, 128:]
    bias = allowed_pairs(segc_ref, segr_ref)
    kinds = []
    for start in range(0, side, 128):
        piece = qkv_ref[:, width + start : width + start + 128]
        piece = (piece * cos_t + turned_half(piece) * sin_t).astype(BF16)
        kr_ref[:, start : start + 128] = piece
        kinds.append(piece)
    values = qkv_ref[:, width + side :].astype(BF16)
    v_ref[...] = values
    for group in range(width // 128):
        piece = qkv_ref[:, group * 128 : group * 128 + 128]
        piece = (piece * cos_t + turned_half(piece) * sin_t).astype(BF16)
        qr_ref[:, group * 128 : group * 128 + 128] = piece
        at = (group % 2) * HEAD_DIM
        key = kinds[group // 2][:, at : at + HEAD_DIM]
        probs = head_probs(stacked_heads(piece), key, bias)
        value = values[:, group * HEAD_DIM : group * HEAD_DIM + HEAD_DIM]
        mixed = contract(probs.astype(BF16), value, ((1,), (0,)))
        o_ref[:, group * 128 : group * 128 + 128] = paired_heads(mixed).astype(BF16)


def attend_back_kernel(
    width, side, do_ref, qr_ref, kr_ref, v_ref, tab_ref, segc_ref, segr_ref, out_ref
):
    cos_t, sin_t = tab_ref[:, :128], tab_ref[:, 128:]
    bias = allowed_pairs(segc_ref, segr_ref)
    key_grads = []
    value_grads = []
    for group in range(width // 128):
        tall_q = stacked_heads(qr_ref[:, group * 128 : group * 128 + 128])
        tall_do = stacked_heads(do_ref[:, group * 128 : group * 128 + 128])
        here = slice(group * HEAD_DIM, group * HEAD_DIM + HEAD_DIM)
        key, value = kr_ref[:, here], v_ref[:, here]
        probs = head_probs(tall_q, key, bias)
        value_grads.append(contract(probs.astype(BF16), tall_do, ((0,), (0,))))
        grad_probs = contract(tall_do, value, ((1,), (1,)))
        kept = jnp.sum(grad_probs * probs, axis=1, keepdims=True)
        grad_scores = (probs * (grad_probs - kept)).astype(BF16)
        grad_q = paired_heads(contract(grad_scores, key, ((1,), (0,)))) * SCALING
        grad_q = grad_q * cos_t - turned_half(grad_q) * sin_t
        out_ref[:, group * 128 : group * 128 + 128] = grad_q.astype(BF16)
        key_grads.append(contract(grad_scores, tall_q, ((0,), (0,))) * SCALING)
    for index in range(side // 128):
        both = jnp.concatenate([key_grads[2 * index], key_grads[2 * index + 1]], axis=1)
        both = both * cos_t - turned_half(both) * sin_t
        at = width + index * 128
        out_ref[:, at : at + 128] = both.astype(BF16)
        both = jnp.concatenate([value_grads[2 * index], value_grads[2 * index + 1]], axis=1)
        at = width + side + index * 128
        out_ref[:, at : at + 128] = both.astype(BF16)


def rows_spec(rows, columns):
    return pl.BlockSpec((rows, columns), lambda block: (block, 0))


def segment_specs(rows):
    return [
        pl.BlockSpec((1, rows, 1), lambda block: (block, 0, 0)),
        pl.BlockSpec((1, 1, rows), lambda block: (block, 0, 0)),
    ]


def attend(qkv, table, segments, width, side):
    blocks, rows = segments.shape

    def kernel(*refs):
        attend_kernel(width, side, *refs)

    return pl.pallas_call(
        kernel,
        grid=(blocks,),
        in_specs=[rows_spec(rows, qkv.shape[1]), rows_spec(rows, 256)] + segment_specs(rows),
        out_specs=[
            rows_spec(rows, width),
            rows_spec(rows, width),
            rows_spec(rows, side),
            rows_spec(rows, side),
        ],
        out_shape=[
            jax.ShapeDtypeStruct((blocks * rows, columns), BF16)
            for columns in (width, width, side, side)
        ],
        name="attend",
    )(qkv, table, segments[:, :, None], segments[:, None, :])


def attend_back(grad_mixed, q_rot, k_rot, values, table, segments, width, side):
    blocks, rows = segments.shape

    def kernel(*refs):
        attend_back_kernel(width, side, *refs)

    return pl.pallas_call(
        kernel,
        grid=(blocks,),
        in_specs=[
            rows_spec(rows, width),
            rows_spec(rows, width),
            rows_spec(rows, side),
            rows_spec(rows, side),
            rows_spec(rows, 256),
        ]
        + segment_specs(rows),
        out_specs=rows_spec(rows, width + 2 * side),
        out_shape=jax.ShapeDtypeStruct((blocks * rows, width + 2 * side), BF16),
        name="attend_back",
    )(grad_mixed, q_rot, k_rot, values, table, segments[:, :, None], segments[:, None, :])


def rope_table(segments):
    rows = segments.shape[1]
    span = jnp.arange(rows, dtype=jnp.int32)
    same = (segments[:, :, None] == segments[:, None, :]) & (span[None, :] < span[:, None])
    pos = jnp.sum(same.astype(jnp.int32), axis=2).reshape(-1)
    steps = jnp.arange(HEAD_DIM // 2, dtype=jnp.int32).astype(F32)
    freq = 10000.0 ** (-2.0 * steps / HEAD_DIM)
    angle = pos.astype(F32)[:, None] * freq[None, :]
    cos_half, sin_half = jnp.cos(angle), jnp.sin(angle)
    return jnp.concatenate([cos_half] * 4 + [sin_half] * 4, axis=1)


def swap(value, axis):
    return lax.ppermute(value, axis, [(0, 1), (1, 0)])


def gather_group(value):
    across = swap(value, "x")
    beside = swap(value, "c")
    beside_across = swap(across, "c")
    return jnp.concatenate([value, across, beside, beside_across], axis=0)


def reduce_group(product, left):
    quarter = left.shape[0] // RANKS
    far = product(left[2 * quarter :]).astype(BF16)
    from_core = swap(far, "c")
    across = product(left[quarter : 2 * quarter]) + from_core[quarter:].astype(F32)
    from_chip = swap(across.astype(BF16), "x")
    own = product(left[:quarter]) + from_core[:quarter].astype(F32)
    return own + from_chip.astype(F32)


def gather_z(value):
    return lax.all_gather(value, "dp", axis=0, tiled=True)


def scatter_z(value):
    return lax.psum_scatter(value, "dp", scatter_dimension=0, tiled=True)


def exchange(value):
    return lax.all_to_all(value, ("x", "c"), 0, 0, tiled=True)


def in_y_order(own, other):
    first = lax.axis_index("y") == 0
    return jnp.where(first, own, other), jnp.where(first, other, own)


def own_columns(value, block):
    parts = [value[:, at : at + block] for at in range(0, value.shape[1], block)]
    return in_y_order(jnp.concatenate(parts[::2], axis=1), jnp.concatenate(parts[1::2], axis=1))


def whole_columns(own, other, block):
    zero, one = in_y_order(own, other)
    parts = []
    for at in range(0, own.shape[1], block):
        parts += [zero[:, at : at + block], one[:, at : at + block]]
    return jnp.concatenate(parts, axis=1)


def gather_pair(value):
    own = gather_z(value)
    return own, swap(own, "y")


def scatter_pair(own, other, right):
    sent = swap(inner_rows(other, right).astype(BF16), "y")
    return scatter_z((inner_rows(own, right) + sent.astype(F32)).astype(BF16))


def heads_by_rank(weight):
    rows, columns = weight.shape
    parts = weight.reshape(rows, columns // (RANKS * HEAD_DIM), RANKS, HEAD_DIM)
    return parts.transpose(2, 0, 1, 3).reshape(RANKS * rows, columns // RANKS)


def heads_from_ranks(value):
    ranks, rows, columns = value.shape
    parts = value.reshape(ranks, rows, columns // HEAD_DIM, HEAD_DIM)
    return parts.transpose(1, 2, 0, 3).reshape(rows, ranks * columns)


def units_by_rank(weight, depth, piece, low, high):
    rows = weight.shape[0]
    parts = weight.reshape(rows, depth, 2, RANKS, piece)[..., low:high]
    return parts.transpose(3, 0, 2, 1, 4).reshape(RANKS * rows, 2 * depth * (high - low))


def units_from_ranks(pieces, depth):
    parts = []
    for value in pieces:
        ranks, rows, columns = value.shape
        parts.append(value.reshape(ranks, rows, 2, depth, columns // (2 * depth)))
    parts = [value.transpose(1, 3, 2, 0, 4) for value in parts]
    return jnp.concatenate(parts, axis=-1).reshape(rows, -1)


def unit(value):
    scale = lax.rsqrt(jnp.mean(value * value, axis=-1, keepdims=True) + EPS)
    return value * scale, scale


def unit_back(normed, scale, grad):
    return scale * (grad - normed * jnp.mean(grad * normed, axis=-1, keepdims=True))


def layer(
    layer_input,
    segment_ids,
    live_counts,
    w_query,
    w_key,
    w_value,
    w_out,
    w_gate,
    w_up,
    w_down,
    attn_gain,
    mlp_gain,
    out_grad,
):
    micro, rows, model = layer_input.shape
    tokens = micro * rows
    owned = w_query.shape[0]
    piece = w_down.shape[0]
    width = w_query.shape[1] // RANKS
    side = w_key.shape[1]
    depth = lax.axis_size("dp")
    block = RANKS * owned
    half = model // 2
    cut = -(-piece // 32) * 16
    chunks = ((0, cut), (cut, piece))
    span = jnp.arange(rows, dtype=jnp.int32)
    valid = (span[None, :] < live_counts).astype(F32).reshape(tokens, 1)

    gain1 = attn_gain.astype(F32)[:, None]
    gain2 = mlp_gain.astype(F32)[:, None]
    scaled = lambda weight, gain: (weight.astype(F32) * gain).astype(BF16)
    side_weights = jnp.concatenate([scaled(w_key, gain1), scaled(w_value, gain1)], axis=1)
    qkv_sent = jnp.concatenate(
        [heads_by_rank(scaled(w_query, gain1)), jnp.tile(side_weights, (RANKS, 1))], axis=1
    )
    w_qkv = gather_pair(exchange(qkv_sent))

    inputs = layer_input.reshape(tokens, model).astype(F32)
    n1, r1 = unit(inputs)
    n1_own, n1_other = own_columns(n1.astype(BF16), block)
    n1_all = gather_group(jnp.concatenate([n1_own, n1_other], axis=1))
    segments = gather_group(segment_ids)
    table = rope_table(segments)

    wo = gather_z(jnp.concatenate(in_y_order(w_out, swap(w_out, "y")), axis=0))
    low_gate, low_up = scaled(w_gate, gain2), scaled(w_up, gain2)
    w_gu = []
    for low, high in chunks:
        sent = [units_by_rank(weight, depth, piece, low, high) for weight in (low_gate, low_up)]
        w_gu.append(gather_pair(exchange(jnp.concatenate(sent, axis=1))))
    wd = [
        jnp.concatenate(in_y_order(*gather_pair(w_down[low:high])), axis=0) for low, high in chunks
    ]
    error = out_grad.reshape(tokens, model).astype(F32) * valid
    error_all = gather_group(error.astype(BF16))

    qkv = forward_dot(n1_all, jnp.concatenate(w_qkv, axis=0))
    mixed, q_rot, k_rot, values = attend(qkv, table, segments, width, side)
    hidden = inputs + reduce_group(lambda left: forward_dot(left, wo), mixed)

    n2, r2 = unit(hidden)
    n2_own, n2_other = own_columns(n2.astype(BF16), block)
    n2_all = gather_group(jnp.concatenate([n2_own, n2_other], axis=1))
    inners, grad_gus, raw_gus, grad_wds = [], [], [], []
    for index in range(len(chunks)):
        gate_up = forward_dot(n2_all, jnp.concatenate(w_gu[index], axis=0))
        units = gate_up.shape[1] // 2
        gate, upward = gate_up[:, :units], gate_up[:, units:]
        sigma = jax.nn.sigmoid(gate)
        silu_gate = gate * sigma
        inner = (silu_gate * upward).astype(BF16)
        own, other = in_y_order(inner[:, : units // 2], inner[:, units // 2 :])
        grad_wds.append(scatter_pair(own, other, error_all))
        grad_inner = against(error_all, wd[index])
        grad_gate = grad_inner * upward * (sigma + gate * sigma * (1.0 - sigma))
        grad_up = grad_inner * silu_gate
        grad_gu = jnp.concatenate([grad_gate.astype(BF16), grad_up.astype(BF16)], axis=1)
        raw = exchange(scatter_pair(n2_all[:, :half], n2_all[:, half:], grad_gu))
        raw_gus.append(raw.reshape(RANKS, owned, 2 * units).astype(F32))
        inners.append(inner)
        grad_gus.append(grad_gu)
    inner = jnp.concatenate(inners, axis=1)
    grad_gu = jnp.concatenate(grad_gus, axis=1)
    wd_all = jnp.concatenate(wd, axis=0)
    gu_own = jnp.concatenate([weight[0] for weight in w_gu], axis=1)
    gu_other = jnp.concatenate([weight[1] for weight in w_gu], axis=1)
    gu_all = jnp.concatenate([gu_own, gu_other], axis=0)

    grad_n2 = reduce_group(lambda left: against(left, gu_all), grad_gu)
    grad_n2 = whole_columns(grad_n2[:, :half], grad_n2[:, half:], block)
    grad_hidden = error + unit_back(n2, r2, grad_n2)
    hidden_all = gather_group(grad_hidden.astype(BF16))
    grad_mixed = against(hidden_all, wo).astype(BF16)
    mixed_own, mixed_other = own_columns(mixed, owned)
    grad_wo = scatter_pair(mixed_own, mixed_other, hidden_all).astype(F32)
    grad_qkv = attend_back(grad_mixed, q_rot, k_rot, values, table, segments, width, side)
    qkv_raw = exchange(scatter_pair(n1_all[:, :half], n1_all[:, half:], grad_qkv))
    grad_n1 = reduce_group(lambda left: against(left, jnp.concatenate(w_qkv, axis=0)), grad_qkv)
    grad_n1 = whole_columns(grad_n1[:, :half], grad_n1[:, half:], block)
    input_grad = (grad_hidden + unit_back(n1, r1, grad_n1)).reshape(micro, rows, model)

    result = hidden + reduce_group(lambda left: forward_dot(left, wd_all), inner)
    layer_output = (result * valid).astype(BF16).reshape(micro, rows, model)

    halves = [raw.shape[2] // 2 for raw in raw_gus]
    raw_gate = units_from_ranks([raw[..., :n] for raw, n in zip(raw_gus, halves)], depth)
    raw_up = units_from_ranks([raw[..., n:] for raw, n in zip(raw_gus, halves)], depth)
    qkv_raw = qkv_raw.reshape(RANKS, owned, width + 2 * side).astype(F32)
    raw_query = heads_from_ranks(qkv_raw[:, :, :width])
    raw_side = jnp.sum(qkv_raw[:, :, width:], axis=0)
    raw_key, raw_value = raw_side[:, :side], raw_side[:, side:]
    row_dot = lambda raw, weight: jnp.sum(raw * weight.astype(F32), axis=1)
    grad_gain1 = row_dot(raw_query, w_query) + row_dot(raw_key, w_key) + row_dot(raw_value, w_value)
    grad_gain2 = row_dot(raw_gate, w_gate) + row_dot(raw_up, w_up)
    return (
        layer_output,
        input_grad,
        raw_query * gain1,
        raw_key * gain1,
        raw_value * gain1,
        grad_wo,
        raw_gate * gain2,
        raw_up * gain2,
        jnp.concatenate(grad_wds, axis=0).astype(F32),
        grad_gain1,
        grad_gain2,
    )


def positions(segment):
    place = jnp.arange(segment.shape[0], dtype=jnp.int32)
    before = jnp.concatenate([segment[:1] - 1, segment[:-1]])
    start = lax.cummax(jnp.where(segment != before, place, 0), axis=0)
    return place - start


def rope_pair(pos):
    steps = jnp.arange(HEAD_DIM // 2, dtype=jnp.int32).astype(F32)
    freq = 10000.0 ** (-2.0 * steps / HEAD_DIM)
    angle = pos.astype(F32)[:, None] * freq[None, :]
    cos_half, sin_half = jnp.cos(angle), jnp.sin(angle)
    return (
        jnp.concatenate([cos_half, cos_half], axis=-1),
        jnp.concatenate([sin_half, sin_half], axis=-1),
    )


def rotate(value, cos_t, sin_t):
    half = HEAD_DIM // 2
    turned = jnp.concatenate([-value[..., half:], value[..., :half]], axis=-1)
    return value * cos_t[:, None, :] + turned * sin_t[:, None, :]


def plain_layer(
    layer_input,
    segment_ids,
    live_counts,
    w_query,
    w_key,
    w_value,
    w_out,
    w_gate,
    w_up,
    w_down,
    attn_gain,
    mlp_gain,
    out_grad,
):
    axes = ("dp", "y", "x", "c")
    rows = layer_input.shape[1]
    group = HEADS // KV_HEADS
    width = HEADS * HEAD_DIM
    span = jnp.arange(rows, dtype=jnp.int32)
    whole = lambda value: lax.all_gather(value, axes, axis=0, tiled=True)
    wq, wk, wv, wo, g1 = [whole(w) for w in (w_query, w_key, w_value, w_out, attn_gain)]
    wg, wu, wd, g2 = [whole(w) for w in (w_gate, w_up, w_down, mlp_gain)]
    gain1, gain2 = g1.astype(F32), g2.astype(F32)
    outputs, input_grads, kept = [], [], []
    gain_sums = [0.0, 0.0]
    for micro in range(MICRO):
        segment = segment_ids[micro]
        valid = (span < live_counts[micro, 0]).astype(F32)[:, None]
        cos_t, sin_t = rope_pair(positions(segment))
        allow = (segment[:, None] == segment[None, :]) & (span[None, :] <= span[:, None])
        inputs = layer_input[micro].astype(F32)
        n1, r1 = unit(inputs)
        h1 = (n1 * gain1).astype(BF16)
        query = forward_dot(h1, wq).reshape(rows, HEADS, HEAD_DIM)
        keys = forward_dot(h1, wk).reshape(rows, KV_HEADS, HEAD_DIM)
        values = forward_dot(h1, wv).astype(BF16).reshape(rows, KV_HEADS, HEAD_DIM)
        q_rot = rotate(query, cos_t, sin_t).astype(BF16).reshape(rows, KV_HEADS, group, HEAD_DIM)
        k_rot = rotate(keys, cos_t, sin_t).astype(BF16)
        scores = jnp.einsum("qkgd,skd->kgqs", q_rot, k_rot, preferred_element_type=F32) * SCALING
        probs = jax.nn.softmax(jnp.where(allow, scores, NEG), axis=-1)
        probs_b = probs.astype(BF16)
        mixed = jnp.einsum("kgqs,skd->qkgd", probs_b, values, preferred_element_type=F32)
        mixed = mixed.reshape(rows, width).astype(BF16)
        hidden = inputs + forward_dot(mixed, wo)
        n2, r2 = unit(hidden)
        h2 = (n2 * gain2).astype(BF16)
        gate, upward = forward_dot(h2, wg), forward_dot(h2, wu)
        sigma = jax.nn.sigmoid(gate)
        inner = (gate * sigma * upward).astype(BF16)
        outputs.append(((hidden + forward_dot(inner, wd)) * valid).astype(BF16))
        error = out_grad[micro].astype(F32) * valid
        error_low = error.astype(BF16)
        grad_inner = against(error_low, wd)
        grad_gate = (grad_inner * upward * (sigma + gate * sigma * (1.0 - sigma))).astype(BF16)
        grad_up = (grad_inner * gate * sigma).astype(BF16)
        grad_h2 = against(grad_gate, wg) + against(grad_up, wu)
        gain_sums[1] += jnp.sum(n2 * grad_h2, axis=0)
        grad_hidden = error + unit_back(n2, r2, grad_h2 * gain2)
        grad_low = grad_hidden.astype(BF16)
        grad_mixed = against(grad_low, wo).astype(BF16).reshape(rows, KV_HEADS, group, HEAD_DIM)
        grad_probs = jnp.einsum("qkgd,skd->kgqs", grad_mixed, values, preferred_element_type=F32)
        kept_sum = jnp.sum(grad_probs * probs, axis=-1, keepdims=True)
        grad_scores = (probs * (grad_probs - kept_sum)).astype(BF16)
        grad_values = jnp.einsum("kgqs,qkgd->skd", probs_b, grad_mixed, preferred_element_type=F32)
        grad_values = grad_values.astype(BF16).reshape(rows, KV_HEADS * HEAD_DIM)
        grad_q = jnp.einsum("kgqs,skd->qkgd", grad_scores, k_rot, preferred_element_type=F32)
        grad_k = jnp.einsum("kgqs,qkgd->skd", grad_scores, q_rot, preferred_element_type=F32)
        grad_q = rotate(grad_q.reshape(rows, HEADS, HEAD_DIM) * SCALING, cos_t, -sin_t)
        grad_q = grad_q.astype(BF16).reshape(rows, width)
        grad_k = rotate(grad_k * SCALING, cos_t, -sin_t)
        grad_k = grad_k.astype(BF16).reshape(rows, KV_HEADS * HEAD_DIM)
        grad_h1 = against(grad_q, wq) + against(grad_k, wk) + against(grad_values, wv)
        gain_sums[0] += jnp.sum(n1 * grad_h1, axis=0)
        input_grads.append(grad_hidden + unit_back(n1, r1, grad_h1 * gain1))
        kept.append(
            (h1, grad_q, grad_k, grad_values, mixed, grad_low)
            + (h2, grad_gate, grad_up, inner, error_low)
        )
    joined = [jnp.concatenate(items, axis=0) for items in zip(*kept)]
    scatter = lambda value: lax.psum_scatter(value, axes, scatter_dimension=0, tiled=True)
    pairs = ((0, 1), (0, 2), (0, 3), (4, 5), (6, 7), (6, 8), (9, 10))
    grads = [scatter(inner_rows(joined[left], joined[right])) for left, right in pairs]
    return (
        jnp.stack(outputs, axis=0),
        jnp.stack(input_grads, axis=0),
        *grads,
        scatter(gain_sums[0]),
        scatter(gain_sums[1]),
    )


def solution(mesh):
    inner, outer = mesh.shape["fsdp"], mesh.shape["dp"]
    grid = Mesh(mesh.devices.reshape(outer, inner // RANKS, 2, 2), ("dp", "y", "x", "c"))
    every = ("dp", "y", "x", "c")
    tokens = P(None, every, None)
    flat = P(None, every)
    weight = P(every, None)
    gain = P(every)
    in_specs = (tokens, flat, flat) + (weight,) * 7 + (gain, gain, tokens)
    out_specs = (tokens, tokens) + (weight,) * 7 + (gain, gain)

    def step(*args):
        whole_heads = args[6].shape[0] == HEAD_DIM * mesh.size
        body = layer if whole_heads and inner == 2 * RANKS else plain_layer
        return jax.shard_map(
            body, mesh=grid, in_specs=in_specs, out_specs=out_specs, check_vma=False
        )(*args)

    return step
```

```python
import jax
import jax.numpy as jnp
from jax import lax
from jax.experimental import pallas as pl
from jax.experimental.pallas import tpu as pltpu
from jax.sharding import Mesh, PartitionSpec as P

HEADS = 32
KV_HEADS = 4
HEAD_DIM = 64
MICRO = 2
RANKS = 4
SCALING = HEAD_DIM ** (-0.5)
EPS = 1e-05
NEG = -1000000000.0
BF16 = jnp.bfloat16
F32 = jnp.float32


def contract(left, right, dims):
    return lax.dot_general(left, right, (dims, ((), ())), preferred_element_type=F32)


def inner_rows(left, right):
    return contract(left, right, ((0,), (0,)))


def against(left, weight):
    return contract(left, weight, ((1,), (1,)))


def forward_dot(left, weight):
    return contract(left, weight, ((1,), (0,)))


def turned_half(value):
    lane = lax.broadcasted_iota(jnp.int32, value.shape, 1)
    width = value.shape[1]
    ahead = pltpu.roll(value, width - HEAD_DIM // 2, axis=1)
    behind = pltpu.roll(value, HEAD_DIM // 2, axis=1)
    return jnp.where(lane % HEAD_DIM < HEAD_DIM // 2, -ahead, behind)


def stacked_heads(pair):
    return jnp.concatenate([pair[:, :HEAD_DIM], pair[:, HEAD_DIM:]], axis=0)


def paired_heads(tall):
    rows = tall.shape[0] // 2
    return jnp.concatenate([tall[:rows], tall[rows:]], axis=1)


def allowed_pairs(segc_ref, segr_ref):
    segc, segr = segc_ref[0], segr_ref[0]
    rows = segc.shape[0]
    later = lax.broadcasted_iota(jnp.int32, (rows, rows), 0)
    earlier = lax.broadcasted_iota(jnp.int32, (rows, rows), 1)
    allow = jnp.logical_and(segc == segr, earlier <= later)
    return jnp.where(allow, 0.0, NEG)


def head_probs(tall_q, key, bias):
    scores = contract(tall_q, key, ((1,), (1,))) * SCALING
    rows = bias.shape[0]
    scores = jnp.concatenate(
        [
            jnp.where(bias < 0.0, bias, scores[:rows]),
            jnp.where(bias < 0.0, bias, scores[rows:]),
        ],
        axis=0,
    )
    top = jnp.max(scores, axis=1, keepdims=True)
    grown = jnp.exp(scores - top)
    return grown / jnp.sum(grown, axis=1, keepdims=True)


def attend_kernel(width, side, qkv_ref, tab_ref, segc_ref, segr_ref, o_ref, qr_ref, kr_ref, v_ref):
    cos_t, sin_t = tab_ref[:, :128], tab_ref[:, 128:]
    bias = allowed_pairs(segc_ref, segr_ref)
    kinds = []
    for start in range(0, side, 128):
        piece = qkv_ref[:, width + start : width + start + 128]
        piece = (piece * cos_t + turned_half(piece) * sin_t).astype(BF16)
        kr_ref[:, start : start + 128] = piece
        kinds.append(piece)
    values = qkv_ref[:, width + side :].astype(BF16)
    v_ref[...] = values
    for group in range(width // 128):
        piece = qkv_ref[:, group * 128 : group * 128 + 128]
        piece = (piece * cos_t + turned_half(piece) * sin_t).astype(BF16)
        qr_ref[:, group * 128 : group * 128 + 128] = piece
        at = (group % 2) * HEAD_DIM
        key = kinds[group // 2][:, at : at + HEAD_DIM]
        probs = head_probs(stacked_heads(piece), key, bias)
        value = values[:, group * HEAD_DIM : group * HEAD_DIM + HEAD_DIM]
        mixed = contract(probs.astype(BF16), value, ((1,), (0,)))
        o_ref[:, group * 128 : group * 128 + 128] = paired_heads(mixed).astype(BF16)


def attend_back_kernel(
    width, side, do_ref, qr_ref, kr_ref, v_ref, tab_ref, segc_ref, segr_ref, out_ref
):
    cos_t, sin_t = tab_ref[:, :128], tab_ref[:, 128:]
    bias = allowed_pairs(segc_ref, segr_ref)
    key_grads = []
    value_grads = []
    for group in range(width // 128):
        tall_q = stacked_heads(qr_ref[:, group * 128 : group * 128 + 128])
        tall_do = stacked_heads(do_ref[:, group * 128 : group * 128 + 128])
        here = slice(group * HEAD_DIM, group * HEAD_DIM + HEAD_DIM)
        key, value = kr_ref[:, here], v_ref[:, here]
        probs = head_probs(tall_q, key, bias)
        value_grads.append(contract(probs.astype(BF16), tall_do, ((0,), (0,))))
        grad_probs = contract(tall_do, value, ((1,), (1,)))
        kept = jnp.sum(grad_probs * probs, axis=1, keepdims=True)
        grad_scores = (probs * (grad_probs - kept)).astype(BF16)
        grad_q = paired_heads(contract(grad_scores, key, ((1,), (0,)))) * SCALING
        grad_q = grad_q * cos_t - turned_half(grad_q) * sin_t
        out_ref[:, group * 128 : group * 128 + 128] = grad_q.astype(BF16)
        key_grads.append(contract(grad_scores, tall_q, ((0,), (0,))) * SCALING)
    for index in range(side // 128):
        both = jnp.concatenate([key_grads[2 * index], key_grads[2 * index + 1]], axis=1)
        both = both * cos_t - turned_half(both) * sin_t
        at = width + index * 128
        out_ref[:, at : at + 128] = both.astype(BF16)
        both = jnp.concatenate([value_grads[2 * index], value_grads[2 * index + 1]], axis=1)
        at = width + side + index * 128
        out_ref[:, at : at + 128] = both.astype(BF16)


def rows_spec(rows, columns):
    return pl.BlockSpec((rows, columns), lambda block: (block, 0))


def segment_specs(rows):
    return [
        pl.BlockSpec((1, rows, 1), lambda block: (block, 0, 0)),
        pl.BlockSpec((1, 1, rows), lambda block: (block, 0, 0)),
    ]


def attend(qkv, table, segments, width, side):
    blocks, rows = segments.shape

    def kernel(*refs):
        attend_kernel(width, side, *refs)

    return pl.pallas_call(
        kernel,
        grid=(blocks,),
        in_specs=[rows_spec(rows, qkv.shape[1]), rows_spec(rows, 256)] + segment_specs(rows),
        out_specs=[
            rows_spec(rows, width),
            rows_spec(rows, width),
            rows_spec(rows, side),
            rows_spec(rows, side),
        ],
        out_shape=[
            jax.ShapeDtypeStruct((blocks * rows, columns), BF16)
            for columns in (width, width, side, side)
        ],
        name="attend",
    )(qkv, table, segments[:, :, None], segments[:, None, :])


def attend_back(grad_mixed, q_rot, k_rot, values, table, segments, width, side):
    blocks, rows = segments.shape

    def kernel(*refs):
        attend_back_kernel(width, side, *refs)

    return pl.pallas_call(
        kernel,
        grid=(blocks,),
        in_specs=[
            rows_spec(rows, width),
            rows_spec(rows, width),
            rows_spec(rows, side),
            rows_spec(rows, side),
            rows_spec(rows, 256),
        ]
        + segment_specs(rows),
        out_specs=rows_spec(rows, width + 2 * side),
        out_shape=jax.ShapeDtypeStruct((blocks * rows, width + 2 * side), BF16),
        name="attend_back",
    )(grad_mixed, q_rot, k_rot, values, table, segments[:, :, None], segments[:, None, :])


def rope_table(segments):
    rows = segments.shape[1]
    span = jnp.arange(rows, dtype=jnp.int32)
    same = (segments[:, :, None] == segments[:, None, :]) & (span[None, :] < span[:, None])
    pos = jnp.sum(same.astype(jnp.int32), axis=2).reshape(-1)
    steps = jnp.arange(HEAD_DIM // 2, dtype=jnp.int32).astype(F32)
    freq = 10000.0 ** (-2.0 * steps / HEAD_DIM)
    angle = pos.astype(F32)[:, None] * freq[None, :]
    cos_half, sin_half = jnp.cos(angle), jnp.sin(angle)
    return jnp.concatenate([cos_half] * 4 + [sin_half] * 4, axis=1)


def swap(value, axis):
    return lax.ppermute(value, axis, [(0, 1), (1, 0)])


def gather_group(value):
    across = swap(value, "x")
    beside = swap(value, "c")
    beside_across = swap(across, "c")
    return jnp.concatenate([value, across, beside, beside_across], axis=0)


def reduce_group(product, left):
    quarter = left.shape[0] // RANKS
    far = product(left[2 * quarter :]).astype(BF16)
    from_core = swap(far, "c")
    across = product(left[quarter : 2 * quarter]) + from_core[quarter:].astype(F32)
    across = across.astype(BF16)
    from_chip = swap(across, "x")
    own = product(left[:quarter]) + from_core[:quarter].astype(F32)
    return own + from_chip.astype(F32), across


def gather_z(value):
    return lax.all_gather(value, "dp", axis=0, tiled=True)


def scatter_z(value):
    return lax.psum_scatter(value, "dp", scatter_dimension=0, tiled=True)


def exchange(value):
    return lax.all_to_all(value, ("x", "c"), 0, 0, tiled=True)


def in_y_order(own, other):
    first = lax.axis_index("y") == 0
    return jnp.where(first, own, other), jnp.where(first, other, own)


def own_columns(value, block):
    parts = [value[:, at : at + block] for at in range(0, value.shape[1], block)]
    return in_y_order(jnp.concatenate(parts[::2], axis=1), jnp.concatenate(parts[1::2], axis=1))


def whole_columns(own, other, block):
    zero, one = in_y_order(own, other)
    parts = []
    for at in range(0, own.shape[1], block):
        parts += [zero[:, at : at + block], one[:, at : at + block]]
    return jnp.concatenate(parts, axis=1)


def gather_pair(value):
    own = gather_z(value)
    return own, swap(own, "y")


def after(value, *earlier):
    return lax.optimization_barrier((value, *earlier))[0]


def sent_rows(other, right):
    return inner_rows(other, right).astype(BF16)


def summed_rows(own, right, sent):
    return scatter_z((inner_rows(own, right) + swap(sent, "y").astype(F32)).astype(BF16))


def heads_by_rank(weight):
    rows, columns = weight.shape
    parts = weight.reshape(rows, columns // (RANKS * HEAD_DIM), RANKS, HEAD_DIM)
    return parts.transpose(2, 0, 1, 3).reshape(RANKS * rows, columns // RANKS)


def heads_from_ranks(value):
    ranks, rows, columns = value.shape
    parts = value.reshape(ranks, rows, columns // HEAD_DIM, HEAD_DIM)
    return parts.transpose(1, 2, 0, 3).reshape(rows, ranks * columns)


def units_by_rank(weight, depth, piece, low, high):
    rows = weight.shape[0]
    parts = weight.reshape(rows, depth, 2, RANKS, piece)[..., low:high]
    return parts.transpose(3, 0, 2, 1, 4).reshape(RANKS * rows, 2 * depth * (high - low))


def units_from_ranks(pieces, depth):
    parts = []
    for value in pieces:
        ranks, rows, columns = value.shape
        parts.append(value.reshape(ranks, rows, 2, depth, columns // (2 * depth)))
    parts = [value.transpose(1, 3, 2, 0, 4) for value in parts]
    return jnp.concatenate(parts, axis=-1).reshape(rows, -1)


def unit(value):
    scale = lax.rsqrt(jnp.mean(value * value, axis=-1, keepdims=True) + EPS)
    return value * scale, scale


def unit_back(normed, scale, grad):
    return scale * (grad - normed * jnp.mean(grad * normed, axis=-1, keepdims=True))


def layer(
    layer_input,
    segment_ids,
    live_counts,
    w_query,
    w_key,
    w_value,
    w_out,
    w_gate,
    w_up,
    w_down,
    attn_gain,
    mlp_gain,
    out_grad,
):
    micro, rows, model = layer_input.shape
    tokens = micro * rows
    owned = w_query.shape[0]
    piece = w_down.shape[0]
    width = w_query.shape[1] // RANKS
    side = w_key.shape[1]
    depth = lax.axis_size("dp")
    block = RANKS * owned
    half = model // 2
    cut = -(-piece // 32) * 16
    chunks = ((0, cut), (cut, piece))
    span = jnp.arange(rows, dtype=jnp.int32)
    valid = (span[None, :] < live_counts).astype(F32).reshape(tokens, 1)

    gain1 = attn_gain.astype(F32)[:, None]
    gain2 = mlp_gain.astype(F32)[:, None]
    scaled = lambda weight, gain: (weight.astype(F32) * gain).astype(BF16)
    side_weights = jnp.concatenate([scaled(w_key, gain1), scaled(w_value, gain1)], axis=1)
    qkv_sent = jnp.concatenate(
        [heads_by_rank(scaled(w_query, gain1)), jnp.tile(side_weights, (RANKS, 1))], axis=1
    )
    w_qkv = gather_pair(exchange(qkv_sent))

    inputs = layer_input.reshape(tokens, model).astype(F32)
    n1, r1 = unit(inputs)
    n1_own, n1_other = own_columns(n1.astype(BF16), block)
    n1_all = gather_group(jnp.concatenate([n1_own, n1_other], axis=1))
    segments = gather_group(segment_ids)
    table = rope_table(segments)

    wo = gather_z(jnp.concatenate(in_y_order(w_out, swap(w_out, "y")), axis=0))
    low_gate, low_up = scaled(w_gate, gain2), scaled(w_up, gain2)
    w_gu = []
    for low, high in chunks:
        sent = [units_by_rank(weight, depth, piece, low, high) for weight in (low_gate, low_up)]
        w_gu.append(gather_pair(exchange(jnp.concatenate(sent, axis=1))))
    wd = [
        jnp.concatenate(in_y_order(*gather_pair(w_down[low:high])), axis=0) for low, high in chunks
    ]
    error = out_grad.reshape(tokens, model).astype(F32) * valid
    error_all = gather_group(error.astype(BF16))

    qkv = forward_dot(n1_all, jnp.concatenate(w_qkv, axis=0))
    mixed, q_rot, k_rot, values = attend(qkv, table, segments, width, side)
    hidden = inputs + reduce_group(lambda left: forward_dot(left, wo), mixed)[0]

    n2, r2 = unit(hidden)
    n2_own, n2_other = own_columns(n2.astype(BF16), block)
    n2_all = gather_group(jnp.concatenate([n2_own, n2_other], axis=1))
    forwards, wd_sides = [], []
    for weights in w_gu:
        gate_up = forward_dot(n2_all, jnp.concatenate(weights, axis=0))
        units = gate_up.shape[1] // 2
        gate, upward = gate_up[:, :units], gate_up[:, units:]
        sigma = jax.nn.sigmoid(gate)
        silu_gate = gate * sigma
        inner = (silu_gate * upward).astype(BF16)
        own, other = in_y_order(inner[:, : units // 2], inner[:, units // 2 :])
        wd_sides.append((own, sent_rows(other, error_all)))
        forwards.append((gate, upward, sigma, silu_gate, inner))
    grad_gus = []
    for index, (gate, upward, sigma, silu_gate, _) in enumerate(forwards):
        grad_inner = against(after(error_all, wd_sides[index][1]), wd[index])
        grad_gate = grad_inner * upward * (sigma + gate * sigma * (1.0 - sigma))
        grad_up = grad_inner * silu_gate
        grad_gus.append(jnp.concatenate([grad_gate.astype(BF16), grad_up.astype(BF16)], axis=1))
    inner = jnp.concatenate([kept[-1] for kept in forwards], axis=1)
    grad_gu = jnp.concatenate(grad_gus, axis=1)
    wd_all = jnp.concatenate(wd, axis=0)
    gu_own = jnp.concatenate([weight[0] for weight in w_gu], axis=1)
    gu_other = jnp.concatenate([weight[1] for weight in w_gu], axis=1)
    gu_all = jnp.concatenate([gu_own, gu_other], axis=0)

    grad_n2, chain = reduce_group(lambda left: against(left, gu_all), grad_gu)
    grad_wds = [summed_rows(own, after(error_all, chain), sent) for own, sent in wd_sides]
    gu_sides = []
    for value in grad_gus:
        value = after(value, chain)
        gu_sides.append((value, sent_rows(n2_all[:, half:], value)))
    grad_n2 = whole_columns(grad_n2[:, :half], grad_n2[:, half:], block)
    grad_hidden = error + unit_back(n2, r2, grad_n2)
    grad_low = grad_hidden.astype(BF16)
    hidden_all = gather_group(grad_low)
    grad_mixed = against(hidden_all, wo).astype(BF16)
    mixed_own, mixed_other = own_columns(mixed, owned)
    wo_sent = sent_rows(mixed_other, hidden_all)
    grad_qkv = attend_back(grad_mixed, q_rot, k_rot, values, table, segments, width, side)
    raw_gus = []
    for (value, sent), earlier in zip(gu_sides, (grad_low, grad_low)):
        raw = exchange(summed_rows(n2_all[:, :half], after(value, earlier), sent))
        raw_gus.append(raw.reshape(RANKS, owned, -1).astype(F32))
    grad_wo = summed_rows(mixed_own, after(hidden_all, grad_qkv), wo_sent).astype(F32)
    qkv_sum = summed_rows(n1_all[:, :half], grad_qkv, sent_rows(n1_all[:, half:], grad_qkv))
    qkv_raw = exchange(qkv_sum)
    qkv_all = jnp.concatenate(w_qkv, axis=0)
    grad_n1, _ = reduce_group(lambda left: against(left, qkv_all), grad_qkv)
    grad_n1 = whole_columns(grad_n1[:, :half], grad_n1[:, half:], block)
    input_grad = (grad_hidden + unit_back(n1, r1, grad_n1)).reshape(micro, rows, model)

    result = hidden + reduce_group(lambda left: forward_dot(left, wd_all), inner)[0]
    layer_output = (result * valid).astype(BF16).reshape(micro, rows, model)

    halves = [raw.shape[2] // 2 for raw in raw_gus]
    raw_gate = units_from_ranks([raw[..., :n] for raw, n in zip(raw_gus, halves)], depth)
    raw_up = units_from_ranks([raw[..., n:] for raw, n in zip(raw_gus, halves)], depth)
    qkv_raw = qkv_raw.reshape(RANKS, owned, width + 2 * side).astype(F32)
    raw_query = heads_from_ranks(qkv_raw[:, :, :width])
    raw_side = jnp.sum(qkv_raw[:, :, width:], axis=0)
    raw_key, raw_value = raw_side[:, :side], raw_side[:, side:]
    row_dot = lambda raw, weight: jnp.sum(raw * weight.astype(F32), axis=1)
    grad_gain1 = row_dot(raw_query, w_query) + row_dot(raw_key, w_key) + row_dot(raw_value, w_value)
    grad_gain2 = row_dot(raw_gate, w_gate) + row_dot(raw_up, w_up)
    return (
        layer_output,
        input_grad,
        raw_query * gain1,
        raw_key * gain1,
        raw_value * gain1,
        grad_wo,
        raw_gate * gain2,
        raw_up * gain2,
        jnp.concatenate(grad_wds, axis=0).astype(F32),
        grad_gain1,
        grad_gain2,
    )


def positions(segment):
    place = jnp.arange(segment.shape[0], dtype=jnp.int32)
    before = jnp.concatenate([segment[:1] - 1, segment[:-1]])
    start = lax.cummax(jnp.where(segment != before, place, 0), axis=0)
    return place - start


def rope_pair(pos):
    steps = jnp.arange(HEAD_DIM // 2, dtype=jnp.int32).astype(F32)
    freq = 10000.0 ** (-2.0 * steps / HEAD_DIM)
    angle = pos.astype(F32)[:, None] * freq[None, :]
    cos_half, sin_half = jnp.cos(angle), jnp.sin(angle)
    return (
        jnp.concatenate([cos_half, cos_half], axis=-1),
        jnp.concatenate([sin_half, sin_half], axis=-1),
    )


def rotate(value, cos_t, sin_t):
    half = HEAD_DIM // 2
    turned = jnp.concatenate([-value[..., half:], value[..., :half]], axis=-1)
    return value * cos_t[:, None, :] + turned * sin_t[:, None, :]


def plain_layer(
    layer_input,
    segment_ids,
    live_counts,
    w_query,
    w_key,
    w_value,
    w_out,
    w_gate,
    w_up,
    w_down,
    attn_gain,
    mlp_gain,
    out_grad,
):
    axes = ("dp", "y", "x", "c")
    rows = layer_input.shape[1]
    group = HEADS // KV_HEADS
    width = HEADS * HEAD_DIM
    span = jnp.arange(rows, dtype=jnp.int32)
    whole = lambda value: lax.all_gather(value, axes, axis=0, tiled=True)
    wq, wk, wv, wo, g1 = [whole(w) for w in (w_query, w_key, w_value, w_out, attn_gain)]
    wg, wu, wd, g2 = [whole(w) for w in (w_gate, w_up, w_down, mlp_gain)]
    gain1, gain2 = g1.astype(F32), g2.astype(F32)
    outputs, input_grads, kept = [], [], []
    gain_sums = [0.0, 0.0]
    for micro in range(MICRO):
        segment = segment_ids[micro]
        valid = (span < live_counts[micro, 0]).astype(F32)[:, None]
        cos_t, sin_t = rope_pair(positions(segment))
        allow = (segment[:, None] == segment[None, :]) & (span[None, :] <= span[:, None])
        inputs = layer_input[micro].astype(F32)
        n1, r1 = unit(inputs)
        h1 = (n1 * gain1).astype(BF16)
        query = forward_dot(h1, wq).reshape(rows, HEADS, HEAD_DIM)
        keys = forward_dot(h1, wk).reshape(rows, KV_HEADS, HEAD_DIM)
        values = forward_dot(h1, wv).astype(BF16).reshape(rows, KV_HEADS, HEAD_DIM)
        q_rot = rotate(query, cos_t, sin_t).astype(BF16).reshape(rows, KV_HEADS, group, HEAD_DIM)
        k_rot = rotate(keys, cos_t, sin_t).astype(BF16)
        scores = jnp.einsum("qkgd,skd->kgqs", q_rot, k_rot, preferred_element_type=F32) * SCALING
        probs = jax.nn.softmax(jnp.where(allow, scores, NEG), axis=-1)
        probs_b = probs.astype(BF16)
        mixed = jnp.einsum("kgqs,skd->qkgd", probs_b, values, preferred_element_type=F32)
        mixed = mixed.reshape(rows, width).astype(BF16)
        hidden = inputs + forward_dot(mixed, wo)
        n2, r2 = unit(hidden)
        h2 = (n2 * gain2).astype(BF16)
        gate, upward = forward_dot(h2, wg), forward_dot(h2, wu)
        sigma = jax.nn.sigmoid(gate)
        inner = (gate * sigma * upward).astype(BF16)
        outputs.append(((hidden + forward_dot(inner, wd)) * valid).astype(BF16))
        error = out_grad[micro].astype(F32) * valid
        error_low = error.astype(BF16)
        grad_inner = against(error_low, wd)
        grad_gate = (grad_inner * upward * (sigma + gate * sigma * (1.0 - sigma))).astype(BF16)
        grad_up = (grad_inner * gate * sigma).astype(BF16)
        grad_h2 = against(grad_gate, wg) + against(grad_up, wu)
        gain_sums[1] += jnp.sum(n2 * grad_h2, axis=0)
        grad_hidden = error + unit_back(n2, r2, grad_h2 * gain2)
        grad_low = grad_hidden.astype(BF16)
        grad_mixed = against(grad_low, wo).astype(BF16).reshape(rows, KV_HEADS, group, HEAD_DIM)
        grad_probs = jnp.einsum("qkgd,skd->kgqs", grad_mixed, values, preferred_element_type=F32)
        kept_sum = jnp.sum(grad_probs * probs, axis=-1, keepdims=True)
        grad_scores = (probs * (grad_probs - kept_sum)).astype(BF16)
        grad_values = jnp.einsum("kgqs,qkgd->skd", probs_b, grad_mixed, preferred_element_type=F32)
        grad_values = grad_values.astype(BF16).reshape(rows, KV_HEADS * HEAD_DIM)
        grad_q = jnp.einsum("kgqs,skd->qkgd", grad_scores, k_rot, preferred_element_type=F32)
        grad_k = jnp.einsum("kgqs,qkgd->skd", grad_scores, q_rot, preferred_element_type=F32)
        grad_q = rotate(grad_q.reshape(rows, HEADS, HEAD_DIM) * SCALING, cos_t, -sin_t)
        grad_q = grad_q.astype(BF16).reshape(rows, width)
        grad_k = rotate(grad_k * SCALING, cos_t, -sin_t)
        grad_k = grad_k.astype(BF16).reshape(rows, KV_HEADS * HEAD_DIM)
        grad_h1 = against(grad_q, wq) + against(grad_k, wk) + against(grad_values, wv)
        gain_sums[0] += jnp.sum(n1 * grad_h1, axis=0)
        input_grads.append(grad_hidden + unit_back(n1, r1, grad_h1 * gain1))
        kept.append(
            (h1, grad_q, grad_k, grad_values, mixed, grad_low)
            + (h2, grad_gate, grad_up, inner, error_low)
        )
    joined = [jnp.concatenate(items, axis=0) for items in zip(*kept)]
    scatter = lambda value: lax.psum_scatter(value, axes, scatter_dimension=0, tiled=True)
    pairs = ((0, 1), (0, 2), (0, 3), (4, 5), (6, 7), (6, 8), (9, 10))
    grads = [scatter(inner_rows(joined[left], joined[right])) for left, right in pairs]
    return (
        jnp.stack(outputs, axis=0),
        jnp.stack(input_grads, axis=0),
        *grads,
        scatter(gain_sums[0]),
        scatter(gain_sums[1]),
    )


def solution(mesh):
    inner, outer = mesh.shape["fsdp"], mesh.shape["dp"]
    grid = Mesh(mesh.devices.reshape(outer, inner // RANKS, 2, 2), ("dp", "y", "x", "c"))
    every = ("dp", "y", "x", "c")
    tokens = P(None, every, None)
    flat = P(None, every)
    weight = P(every, None)
    gain = P(every)
    in_specs = (tokens, flat, flat) + (weight,) * 7 + (gain, gain, tokens)
    out_specs = (tokens, tokens) + (weight,) * 7 + (gain, gain)

    def step(*args):
        whole_heads = args[6].shape[0] == HEAD_DIM * mesh.size
        body = layer if whole_heads and inner == 2 * RANKS else plain_layer
        return jax.shard_map(
            body, mesh=grid, in_specs=in_specs, out_specs=out_specs, check_vma=False
        )(*args)

    return step
```
